32 devices in a mesh: pair: 4 (over z), virt: 8 (over y, x, core).
Axes of the slice: x: 2, y: 2, z: 4, core: 2. Of those that a mesh axis runs over, the one named last changes fastest.
Arguments:
- amplitudes: bfloat16 [4, 8, 2048, 2048], P('pair', None, 'virt'), may hold values from -6 to 6
- factor: bfloat16 [8192, 1024], P('virt'), may hold values from -0.125 to 0.125
- home: int32 [128], replicated, may hold values from 0 to 127, as said below
- domains: int32 [4, 32], P('pair'), may hold values from 0 to 127, as said below
- coupling: bfloat16 [1024, 1024], P('virt'), may hold values from -6 to 6
- hole_weight: bfloat16 [4, 3, 1024], P('pair', None, 'virt'), may hold values from -3 to 3
- virt_energy: float32 [8192], replicated, may hold values from 0.1 to 1
- occ_i: float32 [8], replicated, may hold values from -0.6 to -0.1
- occ_j: float32 [4], P('pair'), may hold values from -0.6 to -0.1
Outputs:
- residual: float32 [4, 8, 2048, 2048], P('pair', None, 'virt')
The draws below stay inside these ranges and needn't reach their ends.
Inputs may be any that keep to these rules, and one draw needn't show every extreme that they name: `home`: a permutation of the virtual tiles; device k of virt stores the factor rows of slots k * 16 to (k + 1) * 16 - 1. `domains`: each row lists 32 distinct virtual tiles; at most 4 of a row's tiles are stored on any one device of virt, and in every row some device stores exactly 4 of them.
All inputs are finite; a program needn't handle non-finite values.
Results may differ from the reference program's by a relative error of at most 0.0033.
Values may be sent and summed in bfloat16 or wider, within the bound.
No kernel may reach another device: no remote copies, remote signals or barrier semaphores. Data moves between devices by JAX's collectives and lax.ppermute only.
A program may use at most 128 MiB of HBM per device.

```python
import jax
import jax.numpy as jnp
from jax import lax

TILE = 64
NV = 8192
NP = 1024
DOM = 32
CAP = 4
NI = 8
VTILES = 128
VT_DEV = 16
NJ = 4
DV = 2048


def domain_tables(key):
    home = jax.random.permutation(jax.random.fold_in(key, 11), VTILES).astype(jnp.int32)

    def one_row(row_key):
        keys = jax.random.split(row_key, 4)
        owner_ranks = jax.random.permutation(keys[0], VTILES // VT_DEV).astype(jnp.int32)
        bases = jax.random.randint(keys[1], (VTILES // VT_DEV,), 0, VT_DEV).astype(jnp.int32)
        picks = jax.random.permutation(keys[2], (VTILES // VT_DEV - 1) * CAP)[:DOM - CAP].astype(jnp.int32)
        holder_pos = jnp.concatenate([jnp.zeros((CAP,), jnp.int32), 1 + picks // CAP])
        within = jnp.concatenate([jnp.arange(CAP, dtype=jnp.int32), picks % CAP])
        holder = owner_ranks[holder_pos]
        slots = holder * VT_DEV + (bases[holder] + within) % VT_DEV
        order = jax.random.permutation(keys[3], DOM)
        return home[slots][order]
    row_keys = jax.random.split(jax.random.fold_in(key, 23), NJ)
    return (home, jax.vmap(one_row)(row_keys).astype(jnp.int32))


def draw_home(key, part):
    return domain_tables(key)[0]


def draw_domains(key, part):
    return domain_tables(key)[1]


def steps_of(rng, shape, pieces, low, high):
    loudness = 1.0
    for dim, parts in pieces:
        steps = jax.random.uniform(jax.random.fold_in(jax.random.fold_in(rng, 6), dim), (parts,), jnp.float32, low / len(pieces), high / len(pieces))
        loudness = loudness * jnp.repeat(jnp.exp(steps), shape[dim] // parts).reshape((-1,) + (1,) * (len(shape) - 1 - dim))
    return loudness


def centred(key, dims, scale, limit, shards=(), held_as=jnp.bfloat16):
    level = steps_of(key, dims, shards, -0.22, 0.18) if shards else 1.0
    entries = jax.random.normal(key, dims, jnp.float32) * scale * level
    return jnp.minimum(jnp.maximum(entries, -limit), limit).astype(held_as)


def setup_inputs(seed: int = 0) -> dict:
    key_of = jax.random.split(jax.random.key(seed), 10)
    return {
        "amplitudes": centred(key_of[0], (NJ, NI, DV, DV), 1.0, 6.0, ((0, 4), (2, 8))),
        "factor": centred(key_of[1], (NV, NP), DV ** -0.5, 0.125, ((0, 8),)),
        "home": draw_home(jax.random.fold_in(key_of[9], 71), 0),
        "domains": draw_domains(jax.random.fold_in(key_of[9], 71), 0),
        "coupling": centred(key_of[4], (NP, NP), 1.0, 6.0, ((0, 8),)),
        "hole_weight": centred(key_of[5], (NJ, 3, NP), 0.5, 3.0, ((0, 4), (2, 8))),
        "virt_energy": jnp.clip(jax.random.uniform(key_of[6], (NV,), jnp.float32, 0.1, 1.0), 0.1, 1.0),
        "occ_i": jnp.clip(jax.random.uniform(key_of[7], (NI,), jnp.float32, -0.6, -0.1), -0.6, -0.1),
        "occ_j": jnp.clip(-0.6 + 0.5 * jax.random.uniform(key_of[8], (NJ,), jnp.float32) ** steps_of(key_of[8], (NJ,), ((0, 4),), -0.2, 0.2), -0.6, -0.1),
    }


def reference(amplitudes, factor, home, domains, coupling, hole_weight, virt_energy, occ_i, occ_j):
    tile_ids = jnp.arange(VTILES, dtype=jnp.int32)
    slot_of = jnp.zeros((VTILES,), jnp.int32).at[home].set(tile_ids)
    tiles = factor.reshape(VTILES, TILE, NP)
    spots = jnp.arange(DV, dtype=jnp.int32)

    def domain_rows(domain_entry_row):
        return tiles[slot_of[domain_entry_row]].reshape(DV, NP)

    def project(args):
        amps_j, domain_entry_row = args
        domain_coefficient = domain_rows(domain_entry_row)

        def single(amp):
            half = jnp.dot(amp, domain_coefficient, preferred_element_type=jnp.float32).astype(jnp.bfloat16)
            return jnp.dot(domain_coefficient.T, half, preferred_element_type=jnp.float32).astype(jnp.bfloat16)

        return lax.map(single, amps_j)

    projected = lax.map(project, (amplitudes, domains))
    empty_block = jnp.zeros_like(projected[:1])
    below_all = jnp.concatenate([empty_block, projected[:-1]], axis=0)
    above_all = jnp.concatenate([projected[1:], empty_block], axis=0)
    core = coupling.T.astype(jnp.float32)

    def finish(args):
        amps_j, domain_entry_row, own, below, above, weight, energy_j = args
        domain_coefficient = domain_rows(domain_entry_row)
        orbitals = domain_entry_row[spots // TILE] * TILE + spots % TILE
        energies = virt_energy[orbitals]
        weight = weight.astype(jnp.float32)
        hole = (weight[0][None, None, :] * below.astype(jnp.float32)
                + weight[1][None, None, :] * own.astype(jnp.float32)
                + weight[2][None, None, :] * above.astype(jnp.float32))
        dressed = (core[None] * own.astype(jnp.float32) + hole).astype(jnp.bfloat16)

        def single(second_arguments):
            amp, dress, energy_i = second_arguments
            back = jnp.dot(domain_coefficient, dress, preferred_element_type=jnp.float32).astype(jnp.bfloat16)
            ladder = jnp.dot(back, domain_coefficient.T, preferred_element_type=jnp.float32)
            shift = energies[:, None] + energies[None, :] - energy_i - energy_j
            return ladder + shift * amp.astype(jnp.float32)

        return lax.map(single, (amps_j, dressed, occ_i))

    return lax.map(finish, (amplitudes, domains, projected, below_all, above_all, hole_weight, occ_j))
```

```python
import functools

import jax
import jax.numpy as jnp
from jax import lax
from jax.experimental import pallas as pl
from jax.experimental.pallas import tpu as pltpu
from jax.sharding import PartitionSpec as P

TILE = 64
CAP = 4
LANES = 128
GRANT = 20 << 20
ANY = pl.BlockSpec(memory_space=pl.ANY)
SMEM = pl.BlockSpec(memory_space=pltpu.SMEM)
VMEM = pl.BlockSpec(memory_space=pltpu.VMEM)
BF16 = jnp.bfloat16
F32 = jnp.float32


def cost(flops, nbytes):
    return pl.CostEstimate(flops=flops, bytes_accessed=nbytes, transcendentals=0)


def pick_kernel(per_device, me_ref, home_ref, domain_ref, factor_ref, own_ref, table_ref, slot_ref, count_ref, sems):
    tiles, peers, length = home_ref.shape[0], count_ref.shape[0], domain_ref.shape[0]

    def note(s, _):
        slot_ref[home_ref[s]] = s
        return 0

    lax.fori_loop(0, tiles, note, 0, unroll=8)
    for h in range(peers):
        count_ref[h] = 0
    for x in range(peers * CAP):
        table_ref[x] = -1
    me = me_ref[0]

    def place(t, _):
        s = slot_ref[domain_ref[t]]
        holder = s // per_device
        c = count_ref[holder]
        table_ref[holder * CAP + c] = t
        count_ref[holder] = c + 1

        @pl.when(holder == me)
        def _():
            pltpu.make_async_copy(factor_ref.at[s - holder * per_device], own_ref.at[c], sems.at[c]).start()

        return 0

    lax.fori_loop(0, length, place, 0, unroll=4)
    for c in range(CAP):

        @pl.when(c < count_ref[me])
        def _():
            pltpu.make_async_copy(factor_ref.at[0], own_ref.at[c], sems.at[c]).wait()


def pick(me, home, domain, factor, peers):
    per_device = factor.shape[0] // TILE
    cols = factor.shape[1]
    return pl.pallas_call(
        functools.partial(pick_kernel, per_device),
        out_shape=(
            jax.ShapeDtypeStruct((CAP, TILE, cols), factor.dtype),
            jax.ShapeDtypeStruct((peers * CAP,), jnp.int32),
        ),
        in_specs=[SMEM, SMEM, SMEM, ANY],
        out_specs=(VMEM, SMEM),
        scratch_shapes=[
            pltpu.SMEM((home.shape[0],), jnp.int32),
            pltpu.SMEM((peers,), jnp.int32),
            pltpu.SemaphoreType.DMA((CAP,)),
        ],
        name="pick",
    )(me, home, domain, factor.reshape(per_device, TILE, cols))


def order_kernel(holder_ref, table_ref, *refs):
    peers = holder_ref.shape[0]
    pieces, out_ref, sems = refs[:peers], refs[peers], refs[peers + 1]
    for k in range(peers):
        for c in range(CAP):
            t = table_ref[holder_ref[k] * CAP + c]

            @pl.when(t >= 0)
            def _():
                pltpu.make_async_copy(
                    pieces[k].at[c], out_ref.at[pl.ds(pl.multiple_of(t * TILE, TILE), TILE)], sems.at[k, c]
                ).start()

    for k in range(peers):
        for c in range(CAP):
            t = table_ref[holder_ref[k] * CAP + c]

            @pl.when(t >= 0)
            def _():
                pltpu.make_async_copy(pieces[k].at[c], out_ref.at[pl.ds(0, TILE)], sems.at[k, c]).wait()


def order(holders, table, pieces, length):
    peers, cols = len(pieces), pieces[0].shape[-1]
    return pl.pallas_call(
        order_kernel,
        out_shape=jax.ShapeDtypeStruct((length * TILE, cols), pieces[0].dtype),
        in_specs=[SMEM, SMEM] + [ANY] * peers,
        out_specs=VMEM,
        scratch_shapes=[pltpu.SemaphoreType.DMA((peers, CAP))],
        cost_estimate=cost(0, 4 * length * TILE * cols),
        name="order",
    )(holders, table, *pieces)


def half_kernel(first, me_ref, amp_ref, dom_ref, *refs):
    *outs, held = refs
    rows, depth = amp_ref.shape[2:]
    width = dom_ref.shape[1] // len(outs)
    count = outs[0].shape[1] // width
    held[...] = jnp.dot(
        amp_ref[0, first : first + count].reshape(count * rows, depth), dom_ref[...], preferred_element_type=F32
    ).astype(BF16)
    for r, out in enumerate(outs):
        cols = pl.ds(pl.multiple_of((me_ref[0] ^ r) * width, width), width)
        for i in range(count):
            out[:, i * width : (i + 1) * width] = held[i * rows : (i + 1) * rows, cols]


def half_of(me, amps, dom, first, count, peers):
    rows, depth = amps.shape[2:]
    cols = dom.shape[1]
    width = cols // peers
    return pl.pallas_call(
        functools.partial(half_kernel, first),
        out_shape=[jax.ShapeDtypeStruct((rows, count * width), BF16)] * peers,
        in_specs=[SMEM, VMEM, VMEM],
        out_specs=[VMEM] * peers,
        scratch_shapes=[pltpu.VMEM((count * rows, cols), BF16)],
        compiler_params=pltpu.CompilerParams(vmem_limit_bytes=GRANT),
        cost_estimate=cost(2 * count * rows * depth * cols, 2 * depth * (count * rows + cols)),
        name="half",
    )(me, amps, dom)


def project_kernel(me_ref, dom_ref, *refs):
    *parts, out, held = refs
    rows = parts[0].shape[0]
    for r, part in enumerate(parts):
        held[pl.ds(pl.multiple_of((me_ref[0] ^ r) * rows, rows), rows)] = part[...]
    out[...] = lax.dot_general(
        dom_ref[...], held[...], (((0,), (0,)), ((), ())), preferred_element_type=F32
    ).astype(out.dtype)


def project(me, dom, parts):
    depth, cols = dom.shape
    wide = parts[0].shape[1]
    return pl.pallas_call(
        project_kernel,
        out_shape=jax.ShapeDtypeStruct((cols, wide), BF16),
        in_specs=[SMEM] + [VMEM] * (1 + len(parts)),
        out_specs=VMEM,
        scratch_shapes=[pltpu.VMEM((depth, wide), BF16)],
        compiler_params=pltpu.CompilerParams(vmem_limit_bytes=GRANT),
        cost_estimate=cost(2 * depth * cols * wide, 2 * depth * (cols + wide)),
        name="project",
    )(me, dom, *parts)


def back_kernel(me_ref, dom_ref, own_ref, near_ref, far_ref, core_ref, weight_ref, *refs):
    *outs, dressed, held = refs
    width = core_ref.shape[1]
    weight = weight_ref[...]
    core = core_ref[...].astype(F32)
    for i in range(own_ref.shape[1] // width):
        cols = slice(i * width, (i + 1) * width)
        own = own_ref[:, cols].astype(F32)
        hole = (
            weight[0:1] * near_ref[:, cols].astype(F32)
            + weight[1:2] * own
            + weight[2:3] * far_ref[:, cols].astype(F32)
        )
        dressed[:, cols] = (core * own + hole).astype(BF16)
    held[...] = jnp.dot(dom_ref[...], dressed[...], preferred_element_type=F32).astype(BF16)
    rows = outs[0].shape[0]
    for r, out in enumerate(outs):
        out[...] = held[pl.ds(pl.multiple_of((me_ref[0] ^ r) * rows, rows), rows)]


def back_of(me, dom, own, near, far, core, weight, peers):
    depth, cols = dom.shape
    wide = own.shape[1]
    return pl.pallas_call(
        back_kernel,
        out_shape=[jax.ShapeDtypeStruct((depth // peers, wide), BF16)] * peers,
        in_specs=[SMEM] + [VMEM] * 6,
        out_specs=[VMEM] * peers,
        scratch_shapes=[pltpu.VMEM((cols, wide), BF16), pltpu.VMEM((depth, wide), BF16)],
        compiler_params=pltpu.CompilerParams(vmem_limit_bytes=GRANT),
        cost_estimate=cost(2 * depth * cols * wide, 2 * depth * (cols + wide)),
        name="back",
    )(me, dom, own, near, far, core, weight)


def ladder_kernel(first, me_ref, occ_ref, dom_ref, amp_ref, row_ref, col_ref, *refs):
    *parts, _, out, held = refs
    rows = amp_ref.shape[2]
    block = out.shape[3]
    count = out.shape[1]

    @pl.when(pl.program_id(0) == 0)
    def _():
        width = parts[0].shape[1] // count
        for r, part in enumerate(parts):
            cols = pl.ds(pl.multiple_of((me_ref[0] ^ r) * width, width), width)
            for i in range(count):
                held[i * rows : (i + 1) * rows, cols] = part[:, i * width : (i + 1) * width]

    here = pl.ds(pl.multiple_of(pl.program_id(0) * block, block), block)
    ladder = lax.dot_general(
        held[...], dom_ref[here, :], (((1,), (1,)), ((), ())), preferred_element_type=F32
    )
    pairs = row_ref[...] + col_ref[:, here]
    last = occ_ref.shape[0] - 1
    for i in range(count):
        shift = pairs - occ_ref[first + i] - occ_ref[last]
        out[0, i] = ladder[i * rows : (i + 1) * rows] + shift * amp_ref[0, first + i, :, here].astype(F32)


def ladder_first(first, *refs):
    ladder_kernel(first, *refs[:-2], None, *refs[-2:])


def ladder_into(so_far, me, occ, dom, amps, row_energy, col_energy, parts, first, count):
    depth, cols = dom.shape
    rows, width = amps.shape[2:]
    steps = 4
    args = [me, occ, dom, amps, row_energy, col_energy, *parts]
    in_specs = [SMEM, SMEM] + [VMEM] * (4 + len(parts))
    body, aliases = ladder_first, {}
    if so_far is not None:
        body, aliases = ladder_kernel, {len(args): 0}
        args.append(so_far)
        in_specs.append(ANY)
    return pl.pallas_call(
        functools.partial(body, first),
        out_shape=jax.ShapeDtypeStruct(amps.shape, F32),
        grid=(steps,),
        in_specs=in_specs,
        out_specs=pl.BlockSpec((1, count, rows, width // steps), lambda n: (0, first // count, 0, n)),
        scratch_shapes=[pltpu.VMEM((count * rows, cols), BF16)],
        input_output_aliases=aliases,
        compiler_params=pltpu.CompilerParams(vmem_limit_bytes=GRANT),
        cost_estimate=cost(2 * count * rows * cols * width, 6 * count * rows * width + 2 * depth * cols),
        name="ladder",
    )(*args)


def exchange(x, r):
    peers = lax.axis_size("virt")
    return lax.ppermute(x, "virt", [(v, v ^ r) for v in range(peers)])


def spread(own, me):
    peers = lax.axis_size("virt")
    bits = [1 << b for b in range(1, peers.bit_length() - 1)]
    held = [own]
    for even, odd in zip(bits, reversed(bits)):
        pairs = [(v, v ^ (odd if v & 1 else even)) for v in range(peers)]
        held = held + [lax.ppermute(h, "virt", pairs) for h in held]
    held = held + [exchange(h, 1) for h in held]

    def whose(device):
        names = [device]
        for even, odd in zip(bits, reversed(bits)):
            names = names + [n ^ jnp.where(device & 1 == 1, odd, even) for n in names]
        return names

    return held, jnp.stack(whose(me) + whose(me ^ 1)).astype(jnp.int32)


def halo(x):
    n = lax.axis_size("pair")
    rounds = []
    for odd in (0, 1):
        to = list(range(n))
        for i in range(odd, n - 1, 2):
            to[i], to[i + 1] = i + 1, i
        rounds.append(lax.ppermute(x, "pair", list(enumerate(to))))
    return rounds


def halo_weights(weight):
    n = lax.axis_size("pair")
    j = lax.axis_index("pair")
    weight = weight.astype(F32)
    below = jnp.where(j > 0, weight[0], 0.0)
    above = jnp.where(j < n - 1, weight[2], 0.0)
    even = j % 2 == 0
    return jnp.stack([jnp.where(even, above, below), weight[1], jnp.where(even, below, above)])


def chunks_of(total):
    size = 2 if total % 2 == 0 else 1
    return [(first, size) for first in range(0, total, size)]


def on_device(amplitudes, factor, home, domains, coupling, hole_weight, virt_energy, occ_i, occ_j):
    peers = lax.axis_size("virt")
    me = lax.axis_index("virt").astype(jnp.int32)
    me1 = me[None]
    domain = domains[0]
    own, table = pick(me1, home, domain, factor, peers)
    pieces, holders = spread(own, me)
    dom = order(holders, table, pieces, domain.shape[0])
    depth, cols = dom.shape
    rows = depth // peers
    chunks = chunks_of(amplitudes.shape[1])
    halves = []
    for first, count in chunks:
        parts = half_of(me1, amplitudes, dom, first, count, peers)
        halves.append([parts[0]] + [exchange(parts[r], r) for r in range(1, peers)])
    core = coupling.T
    weight = halo_weights(hole_weight[0])
    backs = []
    for parts in halves:
        own_block = project(me1, dom, parts)
        near, far = halo(own_block)
        out = back_of(me1, dom, own_block, near, far, core, weight, peers)
        backs.append([out[0]] + [exchange(out[r], r) for r in range(1, peers)])
    tiles = virt_energy.reshape(-1, TILE)
    chosen = domain[:, None] == jnp.arange(tiles.shape[0], dtype=jnp.int32)[None]
    energy = jnp.sum(jnp.where(chosen[:, :, None], tiles[None], 0.0), axis=1)
    mine = lax.dynamic_slice_in_dim(energy, me * (rows // TILE), rows // TILE)
    col_energy, row_energy = energy.reshape(1, depth), mine.reshape(rows, 1)
    occ = jnp.concatenate([occ_i, occ_j])
    out = None
    for (first, count), parts in zip(chunks, backs):
        out = ladder_into(out, me1, occ, dom, amplitudes, row_energy, col_energy, parts, first, count)
    return out


def with_halo(array, sides, width):
    for axis, dim in sides:
        peers, length = (lax.axis_size(axis), array.shape[dim])
        up = [(i, (i + 1) % peers) for i in range(peers - 1)]
        down = [(j, i) for i, j in up]
        last = lax.slice_in_dim(array, length - width, length, axis=dim)
        first = lax.slice_in_dim(array, 0, width, axis=dim)
        before = lax.ppermute(last, axis, up)
        after = lax.ppermute(first, axis, down)
        array = jnp.concatenate([before, array, after], axis=dim)
    return array


def plainly(amplitudes, factor, home, domains, coupling, hole_weight, virt_energy, occ_i, occ_j):
    factor_cols = factor.shape[1]
    per_device = factor.shape[0] // TILE
    tile_total = home.shape[0]
    domain_entry_row = domains[0]
    slot_of = jnp.sum(
        jnp.where(
            home[None, :] == domain_entry_row[:, None],
            jnp.arange(tile_total, dtype=jnp.int32)[None, :],
            0,
        ),
        axis=1,
    )
    holder = slot_of // per_device
    offset = slot_of % per_device
    domain_len = domain_entry_row.shape[0]
    earlier = jnp.arange(domain_len)[None, :] < jnp.arange(domain_len)[:, None]
    same_holder = holder[None, :] == holder[:, None]
    position = jnp.sum((earlier & same_holder).astype(jnp.int32), axis=1)
    locally_owned = holder == lax.axis_index("virt")
    chosen = locally_owned[None, :] & (
        position[None, :] == jnp.arange(CAP, dtype=jnp.int32)[:, None]
    )
    local_slot = jnp.sum(jnp.where(chosen, offset[None, :], 0), axis=1)
    filled = jnp.any(chosen, axis=1)
    own_tiles = factor.reshape(per_device, TILE, factor_cols)
    outgoing = jnp.where(filled[:, None, None], own_tiles[local_slot], jnp.zeros((), factor.dtype))
    arrived = lax.all_gather(outgoing, "virt", axis=0, tiled=True)
    domain_coefficient = arrived[holder * CAP + position].reshape(-1, factor_cols)
    cluster_amplitude = amplitudes[0]
    half = jnp.einsum(
        "hjm,mf->hfj", cluster_amplitude, domain_coefficient, preferred_element_type=jnp.float32
    ).astype(jnp.bfloat16)
    projected = jnp.einsum(
        "iqd,dp->iqp",
        lax.all_to_all(half, "virt", split_axis=1, concat_axis=2, tiled=True),
        domain_coefficient,
        preferred_element_type=jnp.float32,
    ).astype(jnp.bfloat16)
    neighbours = with_halo(projected[None], (("pair", 0),), 1)
    weights = hole_weight[0].astype(jnp.float32)
    hole = (
        weights[0][None, :, None] * neighbours[0].astype(jnp.float32)
        + weights[1][None, :, None] * neighbours[1].astype(jnp.float32)
        + weights[2][None, :, None] * neighbours[2].astype(jnp.float32)
    )
    dressed = (coupling.astype(jnp.float32)[None] * projected.astype(jnp.float32) + hole).astype(
        jnp.bfloat16
    )
    back = jnp.einsum(
        "iqp,ap->iqa", dressed, domain_coefficient, preferred_element_type=jnp.float32
    ).astype(jnp.bfloat16)
    ladder = jnp.einsum(
        "iqa,bq->iab",
        lax.all_to_all(back, "virt", split_axis=2, concat_axis=1, tiled=True),
        domain_coefficient,
        preferred_element_type=jnp.float32,
    )
    rows_here = cluster_amplitude.shape[1]
    domain_width = cluster_amplitude.shape[2]
    spots = jnp.arange(domain_width, dtype=jnp.int32)
    orbitals = domain_entry_row[spots // TILE] * TILE + spots % TILE
    col_energy = virt_energy[orbitals]
    row_energy = lax.dynamic_slice_in_dim(col_energy, lax.axis_index("virt") * rows_here, rows_here)
    shift = row_energy[None, :, None] + col_energy[None, None, :] - occ_i[:, None, None] - occ_j[0]
    return (ladder + shift * cluster_amplitude.astype(jnp.float32))[None]


def fits(mesh, factor):
    peers = mesh.shape["virt"]
    return peers & (peers - 1) == 0 and peers > 1 and factor.shape[-1] % (peers * LANES) == 0


def solution(mesh):
    placed = (
        P("pair", None, "virt", None),
        P("virt", None),
        P(),
        P("pair", None),
        P("virt", None),
        P("pair", None, "virt"),
        P(),
        P(),
        P("pair"),
    )

    def run(amplitudes, factor, *rest):
        body = on_device if fits(mesh, factor) else plainly
        return jax.shard_map(
            body, mesh=mesh, in_specs=placed, out_specs=P("pair", None, "virt", None), check_vma=False
        )(amplitudes, factor, *rest)

    return run
```
